32 devices in a mesh: rep: 8 (over z, x), shard: 4 (over y, core).
Axes of the slice: x: 2, y: 2, z: 4, core: 2. Of those that a mesh axis runs over, the one named last changes fastest.
Arguments:
- inputs: bfloat16 [8, 1024, 768], P('rep', 'shard'), may hold values from -6 to 6
- query_weight: bfloat16 [768, 768], P('shard'), may hold values from -0.21875 to 0.21875
- key_weight: bfloat16 [768, 768], P('shard'), may hold values from -0.21875 to 0.21875
- value_weight: bfloat16 [768, 768], P('shard'), may hold values from -0.21875 to 0.21875
- out_weight: bfloat16 [768, 768], P('shard'), may hold values from -1.75 to 1.75
- query_bias: float32 [768], P('shard'), may hold values from -1 to 1
- key_bias: float32 [768], P('shard'), may hold values from -1 to 1
- value_bias: float32 [768], P('shard'), may hold values from -0.25 to 0.25
- out_bias: float32 [768], P('shard'), may hold values from -1 to 1
- first_gain: float32 [768], P('shard'), may hold values from 0.25 to 1.75
- first_shift: float32 [768], P('shard'), may hold values from -1 to 1
- up_weight: bfloat16 [768, 3072], P('shard'), may hold values from -0.21875 to 0.21875
- up_bias: float32 [3072], P('shard'), may hold values from -1 to 1
- down_weight: bfloat16 [3072, 768], P('shard'), may hold values from -0.109375 to 0.109375
- down_bias: float32 [768], P('shard'), may hold values from -1 to 1
- second_gain: float32 [768], P('shard'), may hold values from 0.25 to 1.75
- second_shift: float32 [768], P('shard'), may hold values from -1 to 1
- out_grad: bfloat16 [8, 1024, 768], P('rep', 'shard'), may hold values from -6 to 6
- segment_ids: int32 [8, 1024], P('rep', 'shard'), may hold values from 0 to 2, never falling along the last dimension, each value on 1 to 512 neighbouring positions
- pad_mask: int32 [8, 1024], P('rep', 'shard'), may hold values 0 or 1
Outputs:
- outputs: bfloat16 [8, 1024, 768], P('rep', 'shard')
- input_grad: float32 [8, 1024, 768], P('rep', 'shard')
- query_weight_grad: float32 [768, 768], P('shard')
- key_weight_grad: float32 [768, 768], P('shard')
- value_weight_grad: float32 [768, 768], P('shard')
- out_weight_grad: float32 [768, 768], P('shard')
- query_bias_grad: float32 [768], P('shard')
- key_bias_grad: float32 [768], P('shard')
- value_bias_grad: float32 [768], P('shard')
- out_bias_grad: float32 [768], P('shard')
- first_gain_grad: float32 [768], P('shard')
- first_shift_grad: float32 [768], P('shard')
- up_weight_grad: float32 [768, 3072], P('shard')
- up_bias_grad: float32 [3072], P('shard')
- down_weight_grad: float32 [3072, 768], P('shard')
- down_bias_grad: float32 [768], P('shard')
- second_gain_grad: float32 [768], P('shard')
- second_shift_grad: float32 [768], P('shard')
The draws below stay inside these ranges and needn't reach their ends.
Inputs may be any that keep to these rules, and one draw needn't show every extreme that they name: `segment_ids`: along each sequence the ids never fall; each of the 3 documents has 1 to 512 tokens, one exactly 512.
All inputs are finite; a program needn't handle non-finite values. No bound on the sum of `pad_mask` on one device may be relied on, other than what follows from the above.
Results may differ from the reference program's by a relative error of at most 0.033.
Values may be sent and summed in bfloat16 or wider, within the bound.
No kernel may reach another device: no remote copies, remote signals or barrier semaphores. Data moves between devices by JAX's collectives and lax.ppermute only.
A program may use at most 192 MiB of HBM per device.

```python
import math
import jax
import jax.numpy as jnp
import numpy as np
from jax import lax

D = 768
HEADS = 12
HEAD_DIM = 64
FF = 3072
SEQ_LEN = 1024
SEQS = 8
SEGS = 3
DOC_MAX = 512


def place_ends(entries, own_key, low, top_value):
    shape = entries.shape
    index_at = [jax.random.randint(jax.random.fold_in(own_key, axis), (), 0, shape[axis]) for axis in range(len(shape))]
    entries = entries.at[tuple(index_at)].set(low)
    longest = shape.index(max(shape))
    index_at[longest] = (index_at[longest] + 1) % shape[longest]
    return entries.at[tuple(index_at)].set(top_value)


def steps_of(key, shape, cuts, smallest, high):
    gain, own = 1.0, jax.random.fold_in(key, 6)
    for axis_at, blocks in cuts:
        steps = jnp.exp(jax.random.uniform(jax.random.fold_in(own, axis_at), (blocks,), jnp.float32, smallest / len(cuts), high / len(cuts)))
        gain = gain * jnp.repeat(steps, shape[axis_at] // blocks).reshape([-1 if axis == axis_at else 1 for axis in range(len(shape))])
    return gain


def profile(number_of, total, limit, lean):
    weights = [(1 << 20) // math.isqrt(grade ** lean) + 1 for grade in range(2, number_of + 1)]
    surplus, counts = total - limit - (number_of - 1), [1] * (number_of - 1)
    while surplus > 0:
        candidates = [i for i in range(number_of - 1) if counts[i] < limit]
        mass, budget = sum([weights[i] for i in candidates]), surplus
        for i in candidates:
            more = min(limit - counts[i], max(1, budget * weights[i] // mass), surplus)
            counts[i] = counts[i] + more
            surplus = surplus - more
    return np.array([limit] + counts)


def uneven(rng, count, total, most, slope):
    if count == 2:
        one = jax.random.randint(rng, (), max(1, total - most), min(most, total - 1) + 1)
        return jnp.stack([one, total - one])
    lengths = jnp.asarray(profile(count, total, most, slope), jnp.int32)
    twos = (count - 1) // 2
    giver, taker = lengths[1:1 + 2 * twos:2], lengths[2:2 + 2 * twos:2]
    margin = jnp.minimum(giver - 1, most - taker)
    moved = jax.random.randint(jax.random.fold_in(rng, 1), (twos,), 0, 1 << 20) % (margin + 1)
    lengths = lengths.at[1:1 + 2 * twos:2].set(giver - moved).at[2:2 + 2 * twos:2].set(taker + moved)
    return lengths[jax.random.permutation(jax.random.fold_in(rng, 2), count)]


def normal_values(own_key, shape, scale, limit, cuts=(), held_as=jnp.bfloat16):
    factor_of = steps_of(own_key, shape, cuts, -0.22, 0.18) if cuts else 1.0
    entries = jax.random.normal(own_key, shape, jnp.float32) * scale * factor_of
    return jnp.minimum(jnp.maximum(entries, -limit), limit).astype(held_as)


def setup_inputs(seed: int = 0) -> dict:
    seeds = jax.random.split(jax.random.key(seed), 21)
    inputs = normal_values(seeds[0], (SEQS, SEQ_LEN, D), 1.0, 6.0, ((0, 8), (1, 4)))
    query_weight = normal_values(seeds[1], (D, D), D ** -0.5, 0.21875, ((0, 4),))
    key_weight = normal_values(seeds[2], (D, D), D ** -0.5, 0.21875, ((0, 4),))
    value_weight = normal_values(seeds[3], (D, D), D ** -0.5, 0.21875, ((0, 4),))
    out_weight = normal_values(seeds[4], (D, D), (max(2, D // 64)) ** -0.5, 1.75, ((0, 4),))
    query_bias = normal_values(seeds[5], (D,), 0.2, 1.0, ((0, 4),), jnp.float32)
    key_bias = normal_values(seeds[6], (D,), 0.2, 1.0, ((0, 4),), jnp.float32)
    value_bias = normal_values(seeds[7], (D,), 0.05, 0.25, ((0, 4),), jnp.float32)
    out_bias = normal_values(seeds[8], (D,), 0.2, 1.0, ((0, 4),), jnp.float32)
    first_gain = jnp.clip(1.0 + 0.15 * jax.random.normal(seeds[9], (D,), jnp.float32), 0.25, 1.75)
    first_shift = normal_values(seeds[10], (D,), 0.2, 1.0, ((0, 4),), jnp.float32)
    up_weight = normal_values(seeds[11], (D, FF), D ** -0.5, 0.21875, ((0, 4),))
    up_bias = normal_values(seeds[12], (FF,), 0.2, 1.0, ((0, 4),), jnp.float32)
    down_weight = normal_values(seeds[13], (FF, D), FF ** -0.5, 0.109375, ((0, 4),))
    down_bias = normal_values(seeds[14], (D,), 0.2, 1.0, ((0, 4),), jnp.float32)
    second_gain = jnp.clip(1.0 + 0.15 * jax.random.normal(seeds[15], (D,), jnp.float32), 0.25, 1.75)
    second_shift = normal_values(seeds[16], (D,), 0.2, 1.0, ((0, 4),), jnp.float32)
    out_grad = normal_values(seeds[17], (SEQS, SEQ_LEN, D), 1.0, 6.0, ((0, 8), (1, 4)))
    segment_ids = jax.vmap(lambda own: jnp.searchsorted(jnp.cumsum(uneven(own, SEGS, SEQ_LEN, DOC_MAX, 2)), jnp.arange(SEQ_LEN), side="right"))(jax.random.split(seeds[18], SEQS)).reshape((SEQS, SEQ_LEN)).astype(jnp.int32)
    pad_mask = place_ends((jax.random.randint(seeds[19], (SEQS, SEQ_LEN), 0, 16) < 15).astype(jnp.int32), jax.random.fold_in(seeds[19], 1), 0, 1)
    return dict(inputs=inputs, query_weight=query_weight, key_weight=key_weight, value_weight=value_weight, out_weight=out_weight, query_bias=query_bias, key_bias=key_bias, value_bias=value_bias, out_bias=out_bias, first_gain=first_gain, first_shift=first_shift, up_weight=up_weight, up_bias=up_bias, down_weight=down_weight, down_bias=down_bias, second_gain=second_gain, second_shift=second_shift, out_grad=out_grad, segment_ids=segment_ids, pad_mask=pad_mask)


EPSILON = 1e-06
ROTARY_BASE = 10000.0
NEG_LARGE = -1e+30

@jax.custom_vjp
def low(v):
    return lax.optimization_barrier(v.astype(jnp.bfloat16)).astype(jnp.float32)

@jax.custom_vjp
def low_back(v):
    return v

def low_keep(v):
    return (low(v), None)

def low_pass(kept, grad):
    return (grad,)

def back_keep(v):
    return (v, None)

def back_low(kept, grad):
    return (low(grad),)
low.defvjp(low_keep, low_pass)
low_back.defvjp(back_keep, back_low)

def product(left, right):
    return jnp.dot(left, right, precision=lax.Precision.HIGHEST, preferred_element_type=jnp.float32)

def rotary_tables(positions, head_size):
    half_size = head_size // 2
    frequency = ROTARY_BASE ** (-(2.0 * jnp.arange(half_size, dtype=jnp.float32)) / head_size)
    angles = positions.astype(jnp.float32)[:, None] * frequency[None, :]
    return (jnp.cos(angles)[:, None, :], jnp.sin(angles)[:, None, :])

def rotate(matrix, cosine_table, sine_table):
    length = matrix.shape[0]
    half_size = cosine_table.shape[-1]
    paired = matrix.reshape(length, -1, half_size, 2)
    first_part = paired[..., 0]
    other_part = paired[..., 1]
    turned = jnp.stack([first_part * cosine_table - other_part * sine_table, first_part * sine_table + other_part * cosine_table], axis=-1)
    return turned.reshape(matrix.shape)

def layer_norm(matrix, gain_row, shift_row):
    centre = lax.optimization_barrier(jnp.mean(matrix, axis=-1, keepdims=True))
    centred = matrix - centre
    spread = lax.optimization_barrier(jnp.mean(centred * centred, axis=-1, keepdims=True))
    return centred * lax.rsqrt(spread + EPSILON) * gain_row + shift_row

def attention(query_low, key_low, value_low, allowed):
    length = query_low.shape[0]
    score_scale = HEAD_DIM ** (-0.5)

    def to_heads(matrix):
        return matrix.reshape(length, HEADS, HEAD_DIM).transpose(1, 0, 2)

    def one_head(triple):
        raw_scores = low_back(product(triple[0], triple[1].T))
        scores = jnp.where(allowed, raw_scores * score_scale, NEG_LARGE)
        row_peak = lax.optimization_barrier(jnp.max(scores, axis=-1, keepdims=True))
        exponent = jnp.exp(scores - row_peak)
        weights_low = low(exponent / lax.optimization_barrier(jnp.sum(exponent, axis=-1, keepdims=True)))
        return product(weights_low, triple[2])
    heads_out = lax.map(jax.checkpoint(one_head), (to_heads(query_low), to_heads(key_low), to_heads(value_low)))
    return heads_out.transpose(1, 0, 2).reshape(length, HEADS * HEAD_DIM)

def layer(inputs_f, params, allowed, cosine_table, sine_table):
    query_weight, key_weight, value_weight, out_weight, query_bias, key_bias, value_bias, out_bias, first_gain, first_shift, up_weight, up_bias, down_weight, down_bias, second_gain, second_shift = params
    queries = low_back(product(inputs_f, query_weight) + query_bias)
    keys_pre = low_back(product(inputs_f, key_weight) + key_bias)
    value_low = low(low_back(product(inputs_f, value_weight) + value_bias))
    query_low = low(rotate(queries, cosine_table, sine_table))
    key_low = low(rotate(keys_pre, cosine_table, sine_table))
    attended = low(low_back(attention(query_low, key_low, value_low, allowed)))
    branch = low_back(product(attended, out_weight) + out_bias)
    summed = inputs_f + branch
    normed = layer_norm(summed, first_gain, first_shift)
    hidden = low_back(product(low(normed), up_weight) + up_bias)
    active = low(jax.nn.gelu(hidden, approximate=False))
    second = low_back(product(active, down_weight) + down_bias)
    return layer_norm(normed + second, second_gain, second_shift)

def reference(inputs, query_weight, key_weight, value_weight, out_weight, query_bias, key_bias, value_bias, out_bias, first_gain, first_shift, up_weight, up_bias, down_weight, down_bias, second_gain, second_shift, out_grad, segment_ids, pad_mask):
    params = tuple((weight_arg.astype(jnp.float32) for weight_arg in (query_weight, key_weight, value_weight, out_weight, query_bias, key_bias, value_bias, out_bias, first_gain, first_shift, up_weight, up_bias, down_weight, down_bias, second_gain, second_shift)))
    places = jnp.arange(SEQ_LEN, dtype=jnp.int32)
    cosine_table, sine_table = rotary_tables(places, HEAD_DIM)

    def one_sequence(totals, items):
        rows_in, grads_in, doc_ids, real_ids = items
        allowed = (doc_ids[:, None] == doc_ids[None, :]) & (real_ids[None, :] == 1) | (places[:, None] == places[None, :])

        def apply_layer(inputs_f, weights):
            return layer(inputs_f, weights, allowed, cosine_table, sine_table)
        result, pullback = jax.vjp(apply_layer, rows_in.astype(jnp.float32), params)
        row_grad, weight_grads = pullback(grads_in.astype(jnp.float32))
        totals = jax.tree.map(lambda first_term, other_term: first_term + other_term, totals, weight_grads)
        return (totals, (result.astype(jnp.bfloat16), row_grad))
    zeroed = jax.tree.map(jnp.zeros_like, params)
    totals, (outputs, input_grad) = lax.scan(one_sequence, zeroed, (inputs, out_grad, segment_ids, pad_mask))
    return (outputs, input_grad, totals[0], totals[1], totals[2], totals[3], totals[4], totals[5], totals[6], totals[7], totals[8], totals[9], totals[10], totals[11], totals[12], totals[13], totals[14], totals[15])
```

```python
from functools import partial

import jax
import jax.numpy as jnp
from jax import lax
from jax.experimental import pallas as pl
from jax.experimental.pallas import tpu as pltpu
from jax.sharding import PartitionSpec as P

HEAD_DIM = 64


EPSILON = 1e-06
ROTARY_BASE = 10000.0
NEG_LARGE = -1e30


def rotary_tables(positions, head_size):
    half_size = head_size // 2
    frequency = ROTARY_BASE ** (-(2.0 * jnp.arange(half_size, dtype=jnp.float32)) / head_size)
    angles = positions.astype(jnp.float32)[:, None] * frequency[None, :]
    return (jnp.cos(angles)[:, None, :], jnp.sin(angles)[:, None, :])


def rotate(matrix, cosine_table, sine_table):
    length = matrix.shape[0]
    half_size = cosine_table.shape[-1]
    paired = matrix.reshape(length, -1, half_size, 2)
    first_part = paired[..., 0]
    other_part = paired[..., 1]
    turned = jnp.stack(
        [
            first_part * cosine_table - other_part * sine_table,
            first_part * sine_table + other_part * cosine_table,
        ],
        axis=-1,
    )
    return turned.reshape(matrix.shape)


def layer_norm(matrix, gain_row, shift_row):
    centre = jnp.mean(matrix, axis=-1, keepdims=True)
    centred = matrix - centre
    spread = jnp.mean(centred * centred, axis=-1, keepdims=True)
    return centred * lax.rsqrt(spread + EPSILON) * gain_row + shift_row


def inner_rows(left, right):
    return lax.dot_general(
        left, right, (((0,), (0,)), ((), ())), preferred_element_type=jnp.float32
    )


def times_transposed(left, right):
    return lax.dot_general(
        left, right, (((1,), (1,)), ((), ())), preferred_element_type=jnp.float32
    )


def to_groups(matrix):
    return matrix.reshape(matrix.shape[0], -1, 2 * HEAD_DIM).transpose(1, 0, 2)


def from_groups(grouped):
    return grouped.transpose(1, 0, 2).reshape(grouped.shape[1], -1)


def pair_heads(matrix):
    return matrix.reshape(matrix.shape[0], 2, HEAD_DIM)


def attend_group(query_rows, key_rows, value_rows, allowed):
    score_scale = HEAD_DIM ** (-0.5)
    raw_scores = jnp.einsum(
        "qhd,khd->hqk",
        pair_heads(query_rows),
        pair_heads(key_rows),
        preferred_element_type=jnp.float32,
    )
    scores = jnp.where(allowed[None], raw_scores * score_scale, NEG_LARGE)
    row_peak = jnp.max(scores, axis=-1, keepdims=True)
    exponent = jnp.exp(scores - row_peak)
    row_total = jnp.sum(exponent, axis=-1, keepdims=True)
    weights_low = (exponent / row_total).astype(jnp.bfloat16)
    attended = jnp.einsum(
        "hqk,khd->qhd", weights_low, pair_heads(value_rows), preferred_element_type=jnp.float32
    )
    return (attended.reshape(query_rows.shape[0], -1), (row_peak + jnp.log(row_total))[..., 0])


def score_terms(query_rows, key_rows, value_rows, grad_rows, log_totals, allowed):
    score_scale = HEAD_DIM ** (-0.5)
    raw_scores = jnp.einsum(
        "qhd,khd->hqk",
        pair_heads(query_rows),
        pair_heads(key_rows),
        preferred_element_type=jnp.float32,
    )
    scores = jnp.where(allowed[None], raw_scores * score_scale, NEG_LARGE)
    probs = jnp.exp(scores - log_totals[:, :, None])
    grad_probs = jnp.einsum(
        "qhd,khd->hqk",
        pair_heads(grad_rows),
        pair_heads(value_rows),
        preferred_element_type=jnp.float32,
    )
    return (probs, grad_probs)


def full_group_grads(query_rows, key_rows, value_rows, grad_rows, log_totals, allowed):
    score_scale = HEAD_DIM ** (-0.5)
    probs, grad_probs = score_terms(
        query_rows, key_rows, value_rows, grad_rows, log_totals, allowed
    )
    deltas = jnp.sum(probs * grad_probs, axis=-1, keepdims=True)
    grad_scores = (probs * (grad_probs - deltas) * score_scale).astype(jnp.bfloat16)
    grad_query = jnp.einsum(
        "hqk,khd->qhd", grad_scores, pair_heads(key_rows), preferred_element_type=jnp.float32
    )
    grad_key = jnp.einsum(
        "hqk,qhd->khd", grad_scores, pair_heads(query_rows), preferred_element_type=jnp.float32
    )
    grad_value = jnp.einsum(
        "hqk,qhd->khd",
        probs.astype(jnp.bfloat16),
        pair_heads(grad_rows),
        preferred_element_type=jnp.float32,
    )
    return (
        grad_query.reshape(query_rows.shape[0], -1),
        grad_key.reshape(key_rows.shape[0], -1),
        grad_value.reshape(key_rows.shape[0], -1),
    )


def project(params, rows_in, cosine_table, sine_table):
    queries = jnp.dot(rows_in, params[0], preferred_element_type=jnp.float32) + params[4]
    keys_pre = jnp.dot(rows_in, params[1], preferred_element_type=jnp.float32) + params[5]
    values = jnp.dot(rows_in, params[2], preferred_element_type=jnp.float32) + params[6]
    query_low = rotate(queries, cosine_table, sine_table).astype(jnp.bfloat16)
    key_low = rotate(keys_pre, cosine_table, sine_table).astype(jnp.bfloat16)
    return (to_groups(query_low), to_groups(key_low), to_groups(values.astype(jnp.bfloat16)))


def finish(params, rows_in, query_groups, key_all, value_all, allowed):

    def one_group(triple):
        return attend_group(triple[0], triple[1], triple[2], allowed)

    attended_groups, log_totals = lax.map(one_group, (query_groups, key_all, value_all))
    attended = from_groups(attended_groups).astype(jnp.bfloat16)
    branch = jnp.dot(attended, params[3], preferred_element_type=jnp.float32) + params[7]
    summed = rows_in.astype(jnp.float32) + branch
    normed = layer_norm(summed, params[8], params[9])
    normed_low = normed.astype(jnp.bfloat16)
    hidden = jnp.dot(normed_low, params[10], preferred_element_type=jnp.float32) + params[11]
    active = jax.nn.gelu(hidden, approximate=False).astype(jnp.bfloat16)
    second = jnp.dot(active, params[12], preferred_element_type=jnp.float32) + params[13]
    total = normed + second
    result = layer_norm(total, params[14], params[15])
    return (log_totals, attended, summed, normed_low, hidden, active, total, result)


def general_plan(
    inputs,
    query_weight,
    key_weight,
    value_weight,
    out_weight,
    query_bias,
    key_bias,
    value_bias,
    out_bias,
    first_gain,
    first_shift,
    up_weight,
    up_bias,
    down_weight,
    down_bias,
    second_gain,
    second_shift,
    out_grad,
    segment_ids,
    pad_mask,
):
    tokens = inputs.shape[1]
    width = inputs.shape[2]
    rows_in = inputs.reshape(tokens, width)
    local_pos = lax.axis_index("shard") * tokens + jnp.arange(tokens, dtype=jnp.int32)
    all_pos = jnp.arange(tokens * lax.axis_size("shard"), dtype=jnp.int32)
    cosine_table, sine_table = rotary_tables(local_pos, HEAD_DIM)
    own_docs = segment_ids.reshape(tokens)
    key_code = jnp.where(pad_mask.reshape(tokens) == 1, own_docs, -1).astype(jnp.bfloat16)
    own_docs_f = own_docs.astype(jnp.float32)
    params = (
        lax.all_gather(query_weight, "shard", axis=0, tiled=True),
        lax.all_gather(key_weight, "shard", axis=0, tiled=True),
        lax.all_gather(value_weight, "shard", axis=0, tiled=True),
        lax.all_gather(out_weight, "shard", axis=0, tiled=True),
        lax.all_gather(query_bias.astype(jnp.bfloat16), "shard", axis=0, tiled=True).astype(
            query_bias.dtype
        ),
        lax.all_gather(key_bias.astype(jnp.bfloat16), "shard", axis=0, tiled=True).astype(
            key_bias.dtype
        ),
        lax.all_gather(value_bias.astype(jnp.bfloat16), "shard", axis=0, tiled=True).astype(
            value_bias.dtype
        ),
        lax.all_gather(out_bias.astype(jnp.bfloat16), "shard", axis=0, tiled=True).astype(
            out_bias.dtype
        ),
        lax.all_gather(first_gain.astype(jnp.bfloat16), "shard", axis=0, tiled=True).astype(
            first_gain.dtype
        ),
        lax.all_gather(first_shift.astype(jnp.bfloat16), "shard", axis=0, tiled=True).astype(
            first_shift.dtype
        ),
        lax.all_gather(up_weight, "shard", axis=0, tiled=True),
        lax.all_gather(up_bias.astype(jnp.bfloat16), "shard", axis=0, tiled=True).astype(
            up_bias.dtype
        ),
        lax.all_gather(down_weight, "shard", axis=0, tiled=True),
        lax.all_gather(down_bias.astype(jnp.bfloat16), "shard", axis=0, tiled=True).astype(
            down_bias.dtype
        ),
        lax.all_gather(second_gain.astype(jnp.bfloat16), "shard", axis=0, tiled=True).astype(
            second_gain.dtype
        ),
        lax.all_gather(second_shift.astype(jnp.bfloat16), "shard", axis=0, tiled=True).astype(
            second_shift.dtype
        ),
    )
    query_groups, key_groups, value_groups = project(params, rows_in, cosine_table, sine_table)
    key_all, value_all, code_all = (
        lax.all_gather(key_groups, "shard", axis=1, tiled=True),
        lax.all_gather(value_groups, "shard", axis=1, tiled=True),
        lax.all_gather(key_code, "shard", axis=0, tiled=True),
    )
    allowed = (code_all.astype(jnp.float32)[None, :] == own_docs_f[:, None]) | (
        all_pos[None, :] == local_pos[:, None]
    )
    kept = finish(params, rows_in, query_groups, key_all, value_all, allowed)
    outputs = kept[7].astype(jnp.bfloat16).reshape(1, tokens, width)
    params = (
        lax.all_gather(query_weight, "shard", axis=0, tiled=True),
        lax.all_gather(key_weight, "shard", axis=0, tiled=True),
        lax.all_gather(value_weight, "shard", axis=0, tiled=True),
        lax.all_gather(out_weight, "shard", axis=0, tiled=True),
        lax.all_gather(query_bias.astype(jnp.bfloat16), "shard", axis=0, tiled=True).astype(
            query_bias.dtype
        ),
        lax.all_gather(key_bias.astype(jnp.bfloat16), "shard", axis=0, tiled=True).astype(
            key_bias.dtype
        ),
        lax.all_gather(value_bias.astype(jnp.bfloat16), "shard", axis=0, tiled=True).astype(
            value_bias.dtype
        ),
        lax.all_gather(out_bias.astype(jnp.bfloat16), "shard", axis=0, tiled=True).astype(
            out_bias.dtype
        ),
        lax.all_gather(first_gain.astype(jnp.bfloat16), "shard", axis=0, tiled=True).astype(
            first_gain.dtype
        ),
        lax.all_gather(first_shift.astype(jnp.bfloat16), "shard", axis=0, tiled=True).astype(
            first_shift.dtype
        ),
        lax.all_gather(up_weight, "shard", axis=0, tiled=True),
        lax.all_gather(up_bias.astype(jnp.bfloat16), "shard", axis=0, tiled=True).astype(
            up_bias.dtype
        ),
        lax.all_gather(down_weight, "shard", axis=0, tiled=True),
        lax.all_gather(down_bias.astype(jnp.bfloat16), "shard", axis=0, tiled=True).astype(
            down_bias.dtype
        ),
        lax.all_gather(second_gain.astype(jnp.bfloat16), "shard", axis=0, tiled=True).astype(
            second_gain.dtype
        ),
        lax.all_gather(second_shift.astype(jnp.bfloat16), "shard", axis=0, tiled=True).astype(
            second_shift.dtype
        ),
    )
    query_groups, key_groups, value_groups = project(params, rows_in, cosine_table, sine_table)
    key_all, value_all, code_all = (
        lax.all_gather(key_groups, "shard", axis=1, tiled=True),
        lax.all_gather(value_groups, "shard", axis=1, tiled=True),
        lax.all_gather(key_code, "shard", axis=0, tiled=True),
    )
    allowed = (code_all.astype(jnp.float32)[None, :] == own_docs_f[:, None]) | (
        all_pos[None, :] == local_pos[:, None]
    )
    kept = finish(params, rows_in, query_groups, key_all, value_all, allowed)
    log_totals, attended, summed, normed_low, hidden, active, total, result = kept
    grad_rows = out_grad.reshape(tokens, width).astype(jnp.float32)
    unused_second, second_back = jax.vjp(layer_norm, total, params[14], params[15])
    grad_total, grad_second_gain, grad_second_shift = second_back(grad_rows)
    grad_second = grad_total.astype(jnp.bfloat16)
    grad_down_bias = jnp.sum(grad_second.astype(jnp.float32), axis=0)
    grad_down_weight = inner_rows(active, grad_second)
    grad_active = times_transposed(grad_second, params[12])
    unused_gelu, gelu_back = jax.vjp(partial(jax.nn.gelu, approximate=False), hidden)
    grad_hidden = gelu_back(grad_active)[0].astype(jnp.bfloat16)
    grad_up_bias = jnp.sum(grad_hidden.astype(jnp.float32), axis=0)
    grad_up_weight = inner_rows(normed_low, grad_hidden)
    grad_normed = grad_total + times_transposed(grad_hidden, params[10])
    unused_first, first_back = jax.vjp(layer_norm, summed, params[8], params[9])
    grad_summed, grad_first_gain, grad_first_shift = first_back(grad_normed)
    grad_branch = grad_summed.astype(jnp.bfloat16)
    grad_out_bias = jnp.sum(grad_branch.astype(jnp.float32), axis=0)
    grad_out_weight = inner_rows(attended, grad_branch)
    grad_attended = times_transposed(grad_branch, params[3]).astype(jnp.bfloat16)
    grad_groups = to_groups(grad_attended)

    def back_group(items):
        return full_group_grads(items[0], items[1], items[2], items[3], items[4], allowed)

    grad_query_groups, key_terms, value_terms = lax.map(
        back_group, (query_groups, key_all, value_all, grad_groups, log_totals)
    )
    grad_key_groups, grad_value_groups = (
        lax.psum_scatter(
            key_terms.astype(jnp.bfloat16), "shard", scatter_dimension=1, tiled=True
        ).astype(jnp.float32),
        lax.psum_scatter(
            value_terms.astype(jnp.bfloat16), "shard", scatter_dimension=1, tiled=True
        ).astype(jnp.float32),
    )
    grad_queries = rotate(from_groups(grad_query_groups), cosine_table, -sine_table).astype(
        jnp.bfloat16
    )
    grad_keys = rotate(from_groups(grad_key_groups), cosine_table, -sine_table).astype(jnp.bfloat16)
    grad_values = from_groups(grad_value_groups).astype(jnp.bfloat16)
    grad_query_bias = jnp.sum(grad_queries.astype(jnp.float32), axis=0)
    grad_key_bias = jnp.sum(grad_keys.astype(jnp.float32), axis=0)
    grad_value_bias = jnp.sum(grad_values.astype(jnp.float32), axis=0)
    grad_query_weight = inner_rows(rows_in, grad_queries)
    grad_key_weight = inner_rows(rows_in, grad_keys)
    grad_value_weight = inner_rows(rows_in, grad_values)
    input_grad = (
        grad_summed
        + times_transposed(grad_queries, params[0])
        + times_transposed(grad_keys, params[1])
        + times_transposed(grad_values, params[2])
    )
    group_sums = (
        lax.psum_scatter(
            grad_query_weight.astype(jnp.bfloat16), "shard", scatter_dimension=0, tiled=True
        ).astype(jnp.float32),
        lax.psum_scatter(
            grad_key_weight.astype(jnp.bfloat16), "shard", scatter_dimension=0, tiled=True
        ).astype(jnp.float32),
        lax.psum_scatter(
            grad_value_weight.astype(jnp.bfloat16), "shard", scatter_dimension=0, tiled=True
        ).astype(jnp.float32),
        lax.psum_scatter(
            grad_out_weight.astype(jnp.bfloat16), "shard", scatter_dimension=0, tiled=True
        ).astype(jnp.float32),
        lax.psum_scatter(
            grad_query_bias.astype(jnp.bfloat16), "shard", scatter_dimension=0, tiled=True
        ).astype(jnp.float32),
        lax.psum_scatter(
            grad_key_bias.astype(jnp.bfloat16), "shard", scatter_dimension=0, tiled=True
        ).astype(jnp.float32),
        lax.psum_scatter(
            grad_value_bias.astype(jnp.bfloat16), "shard", scatter_dimension=0, tiled=True
        ).astype(jnp.float32),
        lax.psum_scatter(
            grad_out_bias.astype(jnp.bfloat16), "shard", scatter_dimension=0, tiled=True
        ).astype(jnp.float32),
        lax.psum_scatter(
            grad_first_gain.astype(jnp.bfloat16), "shard", scatter_dimension=0, tiled=True
        ).astype(jnp.float32),
        lax.psum_scatter(
            grad_first_shift.astype(jnp.bfloat16), "shard", scatter_dimension=0, tiled=True
        ).astype(jnp.float32),
        lax.psum_scatter(
            grad_up_weight.astype(jnp.bfloat16), "shard", scatter_dimension=0, tiled=True
        ).astype(jnp.float32),
        lax.psum_scatter(
            grad_up_bias.astype(jnp.bfloat16), "shard", scatter_dimension=0, tiled=True
        ).astype(jnp.float32),
        lax.psum_scatter(
            grad_down_weight.astype(jnp.bfloat16), "shard", scatter_dimension=0, tiled=True
        ).astype(jnp.float32),
        lax.psum_scatter(
            grad_down_bias.astype(jnp.bfloat16), "shard", scatter_dimension=0, tiled=True
        ).astype(jnp.float32),
        lax.psum_scatter(
            grad_second_gain.astype(jnp.bfloat16), "shard", scatter_dimension=0, tiled=True
        ).astype(jnp.float32),
        lax.psum_scatter(
            grad_second_shift.astype(jnp.bfloat16), "shard", scatter_dimension=0, tiled=True
        ).astype(jnp.float32),
    )
    summed_all = (
        lax.psum(group_sums[0].astype(jnp.bfloat16), "rep").astype(jnp.float32),
        lax.psum(group_sums[1].astype(jnp.bfloat16), "rep").astype(jnp.float32),
        lax.psum(group_sums[2].astype(jnp.bfloat16), "rep").astype(jnp.float32),
        lax.psum(group_sums[3].astype(jnp.bfloat16), "rep").astype(jnp.float32),
        lax.psum(group_sums[4].astype(jnp.bfloat16), "rep").astype(jnp.float32),
        lax.psum(group_sums[5].astype(jnp.bfloat16), "rep").astype(jnp.float32),
        lax.psum(group_sums[6].astype(jnp.bfloat16), "rep").astype(jnp.float32),
        lax.psum(group_sums[7].astype(jnp.bfloat16), "rep").astype(jnp.float32),
        lax.psum(group_sums[8].astype(jnp.bfloat16), "rep").astype(jnp.float32),
        lax.psum(group_sums[9].astype(jnp.bfloat16), "rep").astype(jnp.float32),
        lax.psum(group_sums[10].astype(jnp.bfloat16), "rep").astype(jnp.float32),
        lax.psum(group_sums[11].astype(jnp.bfloat16), "rep").astype(jnp.float32),
        lax.psum(group_sums[12].astype(jnp.bfloat16), "rep").astype(jnp.float32),
        lax.psum(group_sums[13].astype(jnp.bfloat16), "rep").astype(jnp.float32),
        lax.psum(group_sums[14].astype(jnp.bfloat16), "rep").astype(jnp.float32),
        lax.psum(group_sums[15].astype(jnp.bfloat16), "rep").astype(jnp.float32),
    )
    return (
        outputs,
        input_grad.reshape(1, tokens, width),
        summed_all[0],
        summed_all[1],
        summed_all[2],
        summed_all[3],
        summed_all[4],
        summed_all[5],
        summed_all[6],
        summed_all[7],
        summed_all[8],
        summed_all[9],
        summed_all[10],
        summed_all[11],
        summed_all[12],
        summed_all[13],
        summed_all[14],
        summed_all[15],
    )


BLOCK = 256
LOW = jnp.bfloat16
WIDE = jnp.float32


def dot_nn(left, right):
    return lax.dot_general(
        left, right, (((1,), (0,)), ((), ())), preferred_element_type=jnp.float32
    )


def axis_bits(count):
    bits = []
    step = count // 2
    while step:
        bits.append(step)
        step //= 2
    return bits


def swap(value, axis, bit):
    count = lax.axis_size(axis)
    return lax.ppermute(value, axis, [(at, at ^ bit) for at in range(count)])


def slot_offsets(bits):
    offsets = [0]
    for bit in bits:
        offsets = offsets + [at ^ bit for at in offsets]
    return offsets


def gather_slots(value, bits):
    slots = value[None]
    for bit in bits:
        slots = jnp.concatenate([slots, swap(slots, "shard", bit)], axis=0)
    return slots


def scatter_slots(slots, bits):
    for bit in bits[::-1]:
        half = slots.shape[0] // 2
        arrived = swap(slots[half:].astype(LOW), "shard", bit)
        slots = slots[:half].astype(WIDE) + arrived.astype(WIDE)
    return slots[0]


def exchange_slots(slots, bits):
    held = slots[:, None]
    for bit in bits[::-1]:
        half = held.shape[0] // 2
        arrived = swap(held[half:], "shard", bit)
        held = jnp.concatenate([held[:half], arrived], axis=1)
    return held[0]


def pick(blocks, indices):
    return jnp.stack([lax.dynamic_index_in_dim(blocks, at, 0, keepdims=False) for at in indices])


def halve(value, rank, order):
    for bit in order:
        value = value.reshape((2, value.shape[0] // 2) + value.shape[1:])
        mine = (rank // bit) % 2
        sent = lax.dynamic_index_in_dim(value, 1 - mine, 0, keepdims=False)
        kept = lax.dynamic_index_in_dim(value, mine, 0, keepdims=False)
        arrived = swap(sent, "rep", bit)
        value = (kept.astype(WIDE) + arrived.astype(WIDE)).astype(LOW)
    return value[0]


def double(value, rank, order):
    value = value[None]
    for bit in order[::-1]:
        arrived = swap(value, "rep", bit)
        upper = (rank // bit) % 2 == 1
        value = jnp.concatenate(
            [jnp.where(upper, arrived, value), jnp.where(upper, value, arrived)], axis=0
        )
    return value


def turn(matrix, cosine, sine, sign):
    width = matrix.shape[1]
    lane = lax.broadcasted_iota(jnp.int32, matrix.shape, 1)
    following = pltpu.roll(matrix, width - 1, 1)
    leading = pltpu.roll(matrix, 1, 1)
    other = jnp.where(lane % 2 == 0, following, leading)
    if sign > 0:
        return matrix * cosine + other * sine
    return matrix * cosine - other * sine


def lanes_of(table_ref, row, width):
    table = table_ref[pl.ds(row, BLOCK), :]
    return jnp.concatenate([table] * (width // table.shape[1]), axis=1)


def attend_kernel(
    owner_ref, near_ref, x_ref, w_ref, bias_ref, cos_ref, sin_ref, code_ref, doc_ref, out_w_ref,
    part_ref, att_ref, wide_ref, lse_ref, qkv_ref,
    w_scr, heads_scr, mask_scr, peak_scr, total_scr, sum_scr,
):
    slots, rows, width = x_ref.shape
    own = out_w_ref.shape[0]
    heads = own // HEAD_DIM
    length = slots * rows
    blocks = length // BLOCK
    per_slot = rows // BLOCK
    for slot in range(slots):
        w_scr[pl.ds(pl.multiple_of(owner_ref[slot] * own, own), own), :] = w_ref[slot]

    def project(block, carry):
        row = pl.multiple_of(block * BLOCK, BLOCK)
        got = x_ref[block // per_slot, pl.ds(pl.multiple_of(block % per_slot * BLOCK, BLOCK), BLOCK), :]
        made = dot_nn(got, w_scr[...]) + bias_ref[...]
        turned = turn(
            made[:, : 2 * own], lanes_of(cos_ref, row, 2 * own), lanes_of(sin_ref, row, 2 * own), 1
        ).astype(LOW)
        query = turned[:, :own] * jnp.asarray(HEAD_DIM**-0.5, LOW)
        low = jnp.concatenate([query, turned[:, own:], made[:, 2 * own :].astype(LOW)], axis=1)
        qkv_ref[pl.ds(row, BLOCK), :] = low
        for at in range(3 * heads):
            heads_scr[at, pl.ds(row, BLOCK), :] = low[:, at * HEAD_DIM : (at + 1) * HEAD_DIM]
        same = code_ref[pl.ds(row, BLOCK), :] == doc_ref[...]
        place = row + lax.broadcasted_iota(jnp.int32, (BLOCK, length), 0)
        itself = place == lax.broadcasted_iota(jnp.int32, (BLOCK, length), 1)
        mask_scr[pl.ds(row, BLOCK), :] = jnp.where(same | itself, 0.0, NEG_LARGE)
        return carry

    lax.fori_loop(0, blocks, project, 0)

    for head in range(heads):

        def one_block(block, carry):
            row = pl.multiple_of(block * BLOCK, BLOCK)
            query = heads_scr[head, pl.ds(row, BLOCK), :]
            peak_scr[...] = jnp.full_like(peak_scr, NEG_LARGE)
            total_scr[...] = jnp.zeros_like(total_scr)
            sum_scr[...] = jnp.zeros_like(sum_scr)

            def one_key(key_block, inner):
                @pl.when(near_ref[block, key_block] == 1)
                def _():
                    at = pl.multiple_of(key_block * BLOCK, BLOCK)
                    keys = heads_scr[heads + head, pl.ds(at, BLOCK), :]
                    values = heads_scr[2 * heads + head, pl.ds(at, BLOCK), :]
                    scores = times_transposed(keys, query) + mask_scr[pl.ds(at, BLOCK), pl.ds(row, BLOCK)]
                    peak = jnp.maximum(peak_scr[...], jnp.max(scores, axis=0, keepdims=True))
                    scale = jnp.exp(peak_scr[...] - peak)
                    weights = jnp.exp(scores - peak)
                    total_scr[...] = total_scr[...] * scale + jnp.sum(weights, axis=0, keepdims=True)
                    sum_scr[...] = sum_scr[...] * scale + inner_rows(values, weights.astype(LOW))
                    peak_scr[...] = peak

                return inner

            lax.fori_loop(0, blocks, one_key, 0)
            result = sum_scr[...] / total_scr[...]
            wide_ref[pl.ds(head * HEAD_DIM, HEAD_DIM), pl.ds(row, BLOCK)] = result
            att_ref[pl.ds(row, BLOCK), head * HEAD_DIM : (head + 1) * HEAD_DIM] = result.T.astype(LOW)
            lse_ref[pl.ds(head, 1), pl.ds(row, BLOCK)] = peak_scr[...] + jnp.log(total_scr[...])
            return carry

        lax.fori_loop(0, blocks, one_block, 0)

    def finish_block(block, carry):
        row = pl.multiple_of(block * BLOCK, BLOCK)
        part_ref[pl.ds(row, BLOCK), :] = dot_nn(att_ref[pl.ds(row, BLOCK), :], out_w_ref[...]).astype(LOW)
        return carry

    lax.fori_loop(0, blocks, finish_block, 0)


def attend_back_kernel(
    owner_ref, near_ref, w_ref, cos_ref, sin_ref, code_ref, doc_ref, out_w_ref, grad_ref,
    wide_ref, lse_ref, qkv_ref,
    part_ref, back_ref, colsum_ref,
    w_scr, heads_scr, mask_scr, delta_scr, dq_scr, dk_scr, dv_scr,
):
    slots, rows, width = grad_ref.shape
    own = out_w_ref.shape[0]
    heads = own // HEAD_DIM
    length = slots * rows
    blocks = length // BLOCK
    per_slot = rows // BLOCK
    for slot in range(slots):
        w_scr[pl.ds(pl.multiple_of(owner_ref[slot] * own, own), own), :] = w_ref[slot]

    def prepare(block, carry):
        row = pl.multiple_of(block * BLOCK, BLOCK)
        got = grad_ref[block // per_slot, pl.ds(pl.multiple_of(block % per_slot * BLOCK, BLOCK), BLOCK), :]
        grad = times_transposed(got, out_w_ref[...]).astype(LOW)
        low = qkv_ref[pl.ds(row, BLOCK), :]
        for at in range(3 * heads):
            heads_scr[at, pl.ds(row, BLOCK), :] = low[:, at * HEAD_DIM : (at + 1) * HEAD_DIM]
        for head in range(heads):
            piece = grad[:, head * HEAD_DIM : (head + 1) * HEAD_DIM]
            heads_scr[3 * heads + head, pl.ds(row, BLOCK), :] = piece
            product = wide_ref[pl.ds(head * HEAD_DIM, HEAD_DIM), pl.ds(row, BLOCK)] * piece.astype(WIDE).T
            delta_scr[pl.ds(head, 1), pl.ds(row, BLOCK)] = jnp.sum(product, axis=0, keepdims=True)
        same = code_ref[pl.ds(row, BLOCK), :] == doc_ref[...]
        place = row + lax.broadcasted_iota(jnp.int32, (BLOCK, length), 0)
        itself = place == lax.broadcasted_iota(jnp.int32, (BLOCK, length), 1)
        mask_scr[pl.ds(row, BLOCK), :] = jnp.where(same | itself, 0.0, NEG_LARGE)
        return carry

    lax.fori_loop(0, blocks, prepare, 0)
    dq_scr[...] = jnp.zeros_like(dq_scr)
    dk_scr[...] = jnp.zeros_like(dk_scr)
    dv_scr[...] = jnp.zeros_like(dv_scr)

    for head in range(heads):

        def one_pair(pair, carry):
            block = pair // blocks
            key_block = pair % blocks

            @pl.when(near_ref[block, key_block] == 1)
            def _():
                row = pl.multiple_of(block * BLOCK, BLOCK)
                at = pl.multiple_of(key_block * BLOCK, BLOCK)
                query = heads_scr[head, pl.ds(row, BLOCK), :]
                keys = heads_scr[heads + head, pl.ds(at, BLOCK), :]
                values = heads_scr[2 * heads + head, pl.ds(at, BLOCK), :]
                grad = heads_scr[3 * heads + head, pl.ds(row, BLOCK), :]
                scores = times_transposed(keys, query) + mask_scr[pl.ds(at, BLOCK), pl.ds(row, BLOCK)]
                probs = jnp.exp(scores - lse_ref[pl.ds(head, 1), pl.ds(row, BLOCK)])
                grad_probs = times_transposed(values, grad)
                grad_scores = (probs * (grad_probs - delta_scr[pl.ds(head, 1), pl.ds(row, BLOCK)])).astype(LOW)
                dv_scr[head, pl.ds(at, BLOCK), :] += dot_nn(probs.astype(LOW), grad)
                dk_scr[head, pl.ds(at, BLOCK), :] += dot_nn(grad_scores, query)
                dq_scr[head, pl.ds(row, BLOCK), :] += inner_rows(grad_scores, keys)

            return carry

        lax.fori_loop(0, blocks * blocks, one_pair, 0)

    colsum_ref[...] = jnp.zeros_like(colsum_ref)

    def finish_block(block, carry):
        row = pl.multiple_of(block * BLOCK, BLOCK)
        turned = jnp.concatenate(
            [dq_scr[head, pl.ds(row, BLOCK), :] * HEAD_DIM**-0.5 for head in range(heads)]
            + [dk_scr[head, pl.ds(row, BLOCK), :] for head in range(heads)],
            axis=1,
        )
        turned = turn(turned, lanes_of(cos_ref, row, 2 * own), lanes_of(sin_ref, row, 2 * own), -1)
        wide = jnp.concatenate(
            [turned] + [dv_scr[head, pl.ds(row, BLOCK), :] for head in range(heads)], axis=1
        )
        low = wide.astype(LOW)
        back_ref[pl.ds(row, BLOCK), :] = low
        colsum_ref[...] += jnp.sum(low.astype(WIDE), axis=0, keepdims=True)
        part_ref[pl.ds(row, BLOCK), :] = times_transposed(low, w_scr[...]).astype(LOW)
        return carry

    lax.fori_loop(0, blocks, finish_block, 0)


def feed_kernel(
    owner_ref, n_ref, up_ref, bias_ref, down_ref, part_ref, act_ref, slope_ref, up_scr
):
    slots, rows, width = n_ref.shape
    own = up_ref.shape[1]
    for slot in range(slots):
        up_scr[pl.ds(pl.multiple_of(owner_ref[slot] * own, own), own), :] = up_ref[slot]

    def one_block(block, carry):
        row = pl.multiple_of(block * rows, rows)
        hidden = dot_nn(n_ref[block], up_scr[...]) + bias_ref[...]
        cdf = 0.5 * (1.0 + lax.erf(hidden * 0.5**0.5))
        density = jnp.exp(-0.5 * hidden * hidden) * (0.5 / jnp.pi) ** 0.5
        active = (hidden * cdf).astype(LOW)
        act_ref[pl.ds(row, rows), :] = active
        slope_ref[pl.ds(row, rows), :] = (cdf + hidden * density).astype(slope_ref.dtype)
        part_ref[pl.ds(row, rows), :] = dot_nn(active, down_ref[...]).astype(LOW)
        return carry

    lax.fori_loop(0, slots, one_block, 0)


def feed_back_kernel(
    owner_ref, g_ref, up_ref, down_ref, slope_ref, part_ref, grad_ref, colsum_ref, up_scr
):
    slots, rows, width = g_ref.shape
    own = up_ref.shape[1]
    for slot in range(slots):
        up_scr[pl.ds(pl.multiple_of(owner_ref[slot] * own, own), own), :] = up_ref[slot]
    colsum_ref[...] = jnp.zeros_like(colsum_ref)

    def one_block(block, carry):
        row = pl.multiple_of(block * rows, rows)
        back = times_transposed(g_ref[block], down_ref[...])
        grad = (back * slope_ref[pl.ds(row, rows), :].astype(WIDE)).astype(LOW)
        grad_ref[pl.ds(row, rows), :] = grad
        colsum_ref[...] += jnp.sum(grad.astype(WIDE), axis=0, keepdims=True)
        part_ref[pl.ds(row, rows), :] = times_transposed(grad, up_scr[...]).astype(LOW)
        return carry

    lax.fori_loop(0, slots, one_block, 0)


def call_kernel(kernel, scalars, outs, scratch, flops, *args):
    vmem = pl.BlockSpec(memory_space=pltpu.VMEM)
    smem = pl.BlockSpec(memory_space=pltpu.SMEM)
    size = sum(a.size * a.dtype.itemsize for a in args) + sum(
        o.size * o.dtype.itemsize for o in outs
    )
    return pl.pallas_call(
        kernel,
        out_shape=tuple(outs),
        in_specs=[smem] * scalars + [vmem] * (len(args) - scalars),
        out_specs=tuple([vmem] * len(outs)),
        scratch_shapes=scratch,
        cost_estimate=pl.CostEstimate(flops=flops, bytes_accessed=size, transcendentals=0),
        compiler_params=pltpu.CompilerParams(vmem_limit_bytes=60 * 1024 * 1024),
    )(*args)


def norm_stats(matrix):
    centred = matrix - jnp.mean(matrix, axis=-1, keepdims=True)
    spread = jnp.mean(centred * centred, axis=-1, keepdims=True)
    scale = lax.rsqrt(spread + EPSILON)
    return centred * scale, scale


def norm_back(grad, unit, scale, gain):
    inner = grad * gain
    along = jnp.mean(inner * unit, axis=-1, keepdims=True)
    level = jnp.mean(inner, axis=-1, keepdims=True)
    return scale * (inner - level - unit * along)


def split_plan(
    inputs, query_weight, key_weight, value_weight, out_weight, query_bias, key_bias, value_bias,
    out_bias, first_gain, first_shift, up_weight, up_bias, down_weight, down_bias, second_gain,
    second_shift, out_grad, segment_ids, pad_mask,
):
    shards = lax.axis_size("shard")
    replicas = lax.axis_size("rep")
    me = lax.axis_index("shard")
    rank = lax.axis_index("rep")
    bits = axis_bits(shards)
    offsets = slot_offsets(bits)
    tokens, width = inputs.shape[1:]
    own = width // shards
    heads = own // HEAD_DIM
    length = tokens * shards
    hidden = up_bias.shape[0]
    blocks = length // BLOCK
    struct = jax.ShapeDtypeStruct
    owners = jnp.stack([me ^ at for at in offsets]).astype(jnp.int32)

    rows_in = inputs.reshape(tokens, width)
    x_slots = gather_slots(rows_in, bits)
    docs = segment_ids.reshape(tokens)
    codes = jnp.where(pad_mask.reshape(tokens) == 1, docs, -1)
    side_rows = [jnp.pad(v.astype(WIDE), (0, width - v.shape[0])) for v in (docs, codes)] + [
        jnp.pad(v, (0, width - own))
        for v in (out_bias, first_gain, first_shift, down_bias, second_gain, second_shift)
    ]
    side = gather_slots(jnp.stack(side_rows).astype(LOW), bits)
    doc_row = side[:, 0, :tokens].astype(WIDE).reshape(1, length)
    code_col = side[:, 1, :tokens].astype(WIDE).reshape(length, 1)
    ordered = pick(side[:, 2:, :own], [jnp.argmax(owners == at) for at in range(shards)])
    vectors = ordered.astype(WIDE).transpose(1, 0, 2).reshape(6, width)
    out_bias_row, gain_1, shift_1, down_bias_row, gain_2, shift_2 = [
        vectors[at : at + 1] for at in range(6)
    ]

    qkv_blocks = (
        jnp.stack([query_weight, key_weight, value_weight], axis=1)
        .reshape(own, 3, shards, own)
        .transpose(2, 0, 1, 3)
        .reshape(shards, own, 3 * own)
    )
    sources = jnp.stack([me ^ at for at in range(shards)]).astype(jnp.int32)
    w_slots = exchange_slots(pick(qkv_blocks, [me ^ at for at in offsets]), bits)
    up_blocks = up_weight.reshape(own, shards, hidden).transpose(1, 0, 2)
    up_slots = exchange_slots(pick(up_blocks, [me ^ at for at in offsets]), bits)
    qkv_bias = jnp.concatenate([query_bias, key_bias, value_bias]).reshape(1, 3 * own)

    places = (owners[:, None] * tokens + jnp.arange(tokens, dtype=jnp.int32)).reshape(length)
    lane = jnp.arange(2 * HEAD_DIM, dtype=jnp.int32) % HEAD_DIM
    half = (lane // 2).astype(WIDE)
    frequency = ROTARY_BASE ** (-(2.0 * half) / HEAD_DIM)
    angles = places.astype(WIDE)[:, None] * frequency[None, :]
    cosine = jnp.cos(angles)
    sine = jnp.where(lane % 2 == 0, -1.0, 1.0)[None, :] * jnp.sin(angles)

    parts = doc_row.reshape(blocks, BLOCK)
    low_doc, high_doc = jnp.min(parts, axis=1), jnp.max(parts, axis=1)
    near = (
        (low_doc[:, None] <= high_doc[None, :]) & (high_doc[:, None] >= low_doc[None, :])
    ).astype(jnp.int32)

    part, attended, wide, lse, qkv = call_kernel(
        attend_kernel,
        2,
        [
            struct((length, width), LOW),
            struct((length, own), LOW),
            struct((own, length), WIDE),
            struct((8, length), WIDE),
            struct((length, 3 * own), LOW),
        ],
        [
            pltpu.VMEM((width, 3 * own), LOW),
            pltpu.VMEM((3 * heads, length, HEAD_DIM), LOW),
            pltpu.VMEM((length, length), WIDE),
            pltpu.VMEM((1, BLOCK), WIDE),
            pltpu.VMEM((1, BLOCK), WIDE),
            pltpu.VMEM((HEAD_DIM, BLOCK), WIDE),
        ],
        2 * length * width * own * 4 + 4 * heads * length * length * HEAD_DIM,
        sources, near, x_slots, w_slots, qkv_bias, cosine, sine, code_col, doc_row, out_weight,
    )
    branch = scatter_slots(part.reshape(shards, tokens, width), bits) + out_bias_row
    summed = rows_in.astype(WIDE) + branch
    unit_1, scale_1 = norm_stats(summed)
    normed = unit_1 * gain_1 + shift_1
    n_slots = gather_slots(normed.astype(LOW), bits)

    part, active, slope = call_kernel(
        feed_kernel,
        1,
        [
            struct((length, width), LOW),
            struct((length, hidden), LOW),
            struct((length, hidden), LOW),
        ],
        [pltpu.VMEM((width, hidden), LOW)],
        4 * length * width * hidden,
        sources, n_slots, up_slots, up_bias.reshape(1, hidden), down_weight,
    )
    second = scatter_slots(part.reshape(shards, tokens, width), bits) + down_bias_row
    total = normed + second
    unit_2, scale_2 = norm_stats(total)
    outputs = (unit_2 * gain_2 + shift_2).astype(LOW)

    grad_rows = out_grad.reshape(tokens, width).astype(WIDE)
    grad_total = norm_back(grad_rows, unit_2, scale_2, gain_2)
    grad_second = grad_total.astype(LOW)
    g_slots = gather_slots(grad_second, bits)
    part, grad_hidden, up_sums = call_kernel(
        feed_back_kernel,
        1,
        [
            struct((length, width), LOW),
            struct((length, hidden), LOW),
            struct((1, hidden), WIDE),
        ],
        [pltpu.VMEM((width, hidden), LOW)],
        4 * length * width * hidden,
        sources, g_slots, up_slots, down_weight, slope,
    )
    grad_down = inner_rows(active, g_slots.reshape(length, width)).astype(LOW)
    grad_up = inner_rows(n_slots.reshape(length, width), grad_hidden).astype(LOW)
    grad_normed = grad_total + scatter_slots(part.reshape(shards, tokens, width), bits)
    grad_summed = norm_back(grad_normed, unit_1, scale_1, gain_1)
    grad_branch = grad_summed.astype(LOW)
    b_slots = gather_slots(grad_branch, bits)
    part, back, qkv_sums = call_kernel(
        attend_back_kernel,
        2,
        [
            struct((length, width), LOW),
            struct((length, 3 * own), LOW),
            struct((1, 3 * own), WIDE),
        ],
        [
            pltpu.VMEM((width, 3 * own), LOW),
            pltpu.VMEM((4 * heads, length, HEAD_DIM), LOW),
            pltpu.VMEM((length, length), WIDE),
            pltpu.VMEM((8, length), WIDE),
            pltpu.VMEM((heads, length, HEAD_DIM), WIDE),
            pltpu.VMEM((heads, length, HEAD_DIM), WIDE),
            pltpu.VMEM((heads, length, HEAD_DIM), WIDE),
        ],
        2 * length * width * own * 4 + 10 * heads * length * length * HEAD_DIM,
        sources, near, w_slots, cosine, sine, code_col, doc_row, out_weight, b_slots,
        wide, lse, qkv,
    )
    grad_out = inner_rows(attended, b_slots.reshape(length, width)).astype(LOW)
    grad_qkv = inner_rows(x_slots.reshape(length, width), back).astype(LOW)
    input_grad = grad_summed + scatter_slots(part.reshape(shards, tokens, width), bits)

    order_a = [bit for bit in axis_bits(replicas)[::-1]]
    order_b = order_a[1:2] + order_a[:1] + order_a[2:]
    down_total = double(halve(grad_down.reshape(replicas, -1, width), rank, order_a), rank, order_a)
    down_total = down_total.reshape(hidden, width).astype(WIDE)
    out_total = double(halve(grad_out.reshape(replicas, -1, width), rank, order_a), rank, order_a)
    out_total = out_total.reshape(own, width).astype(WIDE)

    def traded(gradient, order):
        columns = gradient.shape[1]
        pieces = gradient.reshape(shards, replicas, own // replicas, columns).transpose(1, 0, 2, 3)
        piece = halve(pieces, rank, order)
        piece = exchange_slots(pick(piece, [me ^ at for at in offsets]), bits)
        piece = pick(piece, [me ^ at for at in range(shards)])
        return double(piece, rank, order)

    up_total = traded(grad_up, order_b).transpose(0, 2, 1, 3).reshape(own, shards * hidden).astype(WIDE)
    qkv_total = traded(grad_qkv, order_b).transpose(0, 2, 1, 3).reshape(own, shards, 3, own)
    qkv_total = qkv_total.transpose(2, 0, 1, 3).reshape(3, own, width).astype(WIDE)

    def spread(vector):
        pieces = vector.reshape(-1, 1, own)
        mine = (jnp.arange(shards) == me).astype(WIDE)[None, :, None]
        return (pieces * mine).reshape(-1, width)

    def placed(vector):
        pieces = vector.reshape(1, -1)
        mine = (jnp.arange(shards) == me).astype(WIDE)[:, None]
        return (pieces * mine).reshape(-1, width)

    vector_rows = jnp.concatenate(
        [spread(qkv_sums), placed(up_sums)]
        + [
            jnp.sum(rows, axis=0, keepdims=True)
            for rows in (
                grad_branch.astype(WIDE),
                grad_normed * unit_1,
                grad_normed,
                grad_second.astype(WIDE),
                grad_rows * unit_2,
                grad_rows,
            )
        ],
        axis=0,
    )
    for bit in axis_bits(replicas):
        vector_rows = vector_rows + swap(vector_rows, "rep", bit)
    for bit in bits:
        vector_rows = vector_rows + swap(vector_rows, "shard", bit)
    ups = hidden // own
    up_vector = lax.dynamic_slice_in_dim(vector_rows[3 : 3 + ups].reshape(-1), me * hidden, hidden)
    narrow = jnp.concatenate([vector_rows[:3], vector_rows[3 + ups :]], axis=0)
    narrow = lax.dynamic_slice_in_dim(narrow, me * own, own, axis=1)
    return (
        outputs.reshape(1, tokens, width),
        input_grad.reshape(1, tokens, width),
        qkv_total[0],
        qkv_total[1],
        qkv_total[2],
        out_total,
        narrow[0],
        narrow[1],
        narrow[2],
        narrow[3],
        narrow[4],
        narrow[5],
        up_total,
        up_vector,
        down_total,
        narrow[6],
        narrow[7],
        narrow[8],
    )


def solution(mesh):
    shards = mesh.shape["shard"]
    replicas = mesh.shape["rep"]

    def body(*arrays):
        heads = arrays[0].shape[2] // HEAD_DIM
        if heads % shards or shards & (shards - 1) or replicas & (replicas - 1):
            return general_plan(*arrays)
        return split_plan(*arrays)

    return jax.shard_map(
        body,
        mesh=mesh,
        in_specs=(
            P("rep", "shard", None),
            P("shard", None),
            P("shard", None),
            P("shard", None),
            P("shard", None),
            P("shard"),
            P("shard"),
            P("shard"),
            P("shard"),
            P("shard"),
            P("shard"),
            P("shard", None),
            P("shard"),
            P("shard", None),
            P("shard"),
            P("shard"),
            P("shard"),
            P("rep", "shard", None),
            P("rep", "shard"),
            P("rep", "shard"),
        ),
        out_specs=(
            P("rep", "shard", None),
            P("rep", "shard", None),
            P("shard", None),
            P("shard", None),
            P("shard", None),
            P("shard", None),
            P("shard"),
            P("shard"),
            P("shard"),
            P("shard"),
            P("shard"),
            P("shard"),
            P("shard", None),
            P("shard"),
            P("shard", None),
            P("shard"),
            P("shard"),
            P("shard"),
        ),
        check_vma=False,
    )
```
